512 devices in a mesh: ctx: 32 (over z, core), ch: 16 (over x, y).
Axes of the slice: x: 4, y: 4, z: 16, core: 2. Of those that a mesh axis runs over, the one named last changes fastest.
Arguments:
- signal: bfloat16 [4096, 8192], P('ctx', 'ch'), may hold values from -170 to 170, as said below
- norm_gain: float32 [8192], P('ch'), may hold values from 0.1 to 1.9
- skip_gain: float32 [8192], P('ch'), may hold values from 0.5 to 1.5
- filter_taps: bfloat16 [4096, 8192], P('ctx', 'ch'), may hold values from -1.5 to 1.5, as said below
- out_gate: bfloat16 [4096, 8192], P('ctx', 'ch'), may hold values from -6 to 6
Outputs:
- mixture: bfloat16 [4096, 8192], P('ctx', 'ch')
The draws below stay inside these ranges and needn't reach their ends.
Inputs may be any that keep to these rules, and one draw needn't show every extreme that they name: `signal`: features whose channels and tokens have different scales. `filter_taps`: a filter whose taps fall off along the lags at a rate that differs between channels.
All inputs are finite; a program needn't handle non-finite values.
Results may differ from the reference program's by a relative error of at most 0.006.
Values may be sent and summed in bfloat16 or wider, within the bound.
A program may use at most 64 MiB of HBM per device.

```python
import math
import jax
import jax.numpy as jnp
from jax import lax

C = 8192
LENGTH = 4096


def draw_signal(key, part):
    noise_key = jax.random.fold_in(key, 3)
    row_key = jax.random.fold_in(key, 5)
    noise_draw = jnp.clip(jax.random.normal(noise_key, (LENGTH, C), jnp.float32), -5.0, 5.0)
    column = jnp.exp(math.log(10.0) * jnp.arange(C, dtype=jnp.float32) / C) / 3.0
    row_scale = jnp.exp(jax.random.uniform(row_key, (LENGTH, 1), jnp.float32, 0.0, math.log(10.0)))
    return (noise_draw * row_scale * column[None, :]).astype(jnp.bfloat16)


def draw_filter_taps(key, part):
    decay_key = jax.random.fold_in(key, 7)
    noise_key = jax.random.fold_in(key, 11)
    longest = math.log(32.0 * LENGTH)
    log_decay = jax.random.uniform(decay_key, (C,), jnp.float32, math.log(30.0), longest)
    noise_draw = jnp.clip(jax.random.normal(noise_key, (LENGTH, C), jnp.float32), -5.0, 5.0)
    decay_len = jnp.exp(log_decay)
    lag_pos = jnp.arange(LENGTH, dtype=jnp.float32)
    amplitude = 1.0 / jnp.sqrt(0.5 * jnp.minimum(decay_len, 2.0 * LENGTH))
    return (noise_draw * jnp.exp(-lag_pos[:, None] / decay_len[None, :]) * amplitude[None, :]).astype(jnp.bfloat16)


def steps_of(stream_key, dims, pieces, smallest, largest):
    gain, own = 1.0, jax.random.fold_in(stream_key, 6)
    for position, shards_of in pieces:
        draws = jnp.exp(jax.random.uniform(jax.random.fold_in(own, position), (shards_of,), jnp.float32, smallest / len(pieces), largest / len(pieces)))
        gain = gain * jnp.repeat(draws, dims[position] // shards_of).reshape([-1 if axis == position else 1 for axis in range(len(dims))])
    return gain


def scatter_about(key, shape, width, limit, cuts=(), kind=jnp.bfloat16):
    entries = jax.random.normal(key, shape, jnp.float32) * width
    if len(cuts) > 0:
        entries = steps_of(key, shape, cuts, -0.22, 0.18) * entries
    return jnp.clip(entries, min=-limit, max=limit).astype(kind)


def setup_inputs(seed: int = 0) -> dict:
    key_list = jax.random.split(jax.random.key(seed), 6)
    signal = draw_signal(jax.random.fold_in(key_list[5], 71), 0)
    norm_gain = jnp.clip(1.0 + 0.18 * jax.random.normal(key_list[1], (C,), jnp.float32), 0.1, 1.9)
    skip_gain = jnp.clip(0.5 + 1.0 * jax.random.uniform(key_list[2], (C,), jnp.float32) ** steps_of(key_list[2], (C,), ((0, 16),), -0.2, 0.2), 0.5, 1.5)
    filter_taps = draw_filter_taps(jax.random.fold_in(key_list[5], 71), 0)
    out_gate = scatter_about(key_list[4], (LENGTH, C), 1.0, 6.0, ((0, 32), (1, 16)))
    return dict(signal=signal, norm_gain=norm_gain, skip_gain=skip_gain, filter_taps=filter_taps, out_gate=out_gate)


EPS = 1e-06

def reference(signal, norm_gain, skip_gain, filter_taps, out_gate):
    values = signal.astype(jnp.float32)
    row_power = lax.optimization_barrier(jnp.mean(values * values, axis=1, keepdims=True))
    normed = (values * lax.rsqrt(row_power + EPS) * norm_gain[None, :]).astype(jnp.bfloat16)
    seq_len = normed.shape[0]
    padded_len = 2 * seq_len
    group_width = 256
    group_count = C // group_width
    signal_groups = normed.astype(jnp.float32).reshape(seq_len, group_count, group_width).transpose(1, 0, 2)
    filter_groups = filter_taps.astype(jnp.float32).reshape(seq_len, group_count, group_width).transpose(1, 0, 2)

    def convolve_group(inputs_pair):
        sig_group, fil_group = inputs_pair
        product = jnp.fft.rfft(sig_group, n=padded_len, axis=0) * jnp.fft.rfft(fil_group, n=padded_len, axis=0)
        return jnp.fft.irfft(product, n=padded_len, axis=0)[:seq_len]
    convolved = lax.map(convolve_group, (signal_groups, filter_groups))
    convolved = convolved.transpose(1, 0, 2).reshape(seq_len, C)
    mixture = out_gate.astype(jnp.float32) * (convolved + skip_gain[None, :] * normed.astype(jnp.float32))
    return mixture.astype(jnp.bfloat16)
```

```python
import functools
import math

import jax
import jax.numpy as jnp
import ml_dtypes
import numpy as np
from jax import lax
from jax.experimental import pallas as pl
from jax.experimental.pallas import tpu as pltpu
from jax.sharding import PartitionSpec as P

C = 8192
EPS = 1e-06
MESH = pl.DeviceIdType.MESH
STEP = 4


def high_low(table):
    high = table.astype(ml_dtypes.bfloat16)
    low = (table - high.astype(np.float64)).astype(ml_dtypes.bfloat16)
    return high, low


def dft_tables(rows):
    span = 2 * rows
    freq = np.arange(rows)
    def phase(a, b):
        return (a[:, None] * b[None, :] % span) * (2.0 * math.pi / span)
    row = np.arange(rows)
    angle = phase(row, freq)
    fwd_im = -np.sin(angle)
    fwd_im[:, 0] = np.cos(math.pi * row)
    forward = np.concatenate([np.cos(angle), fwd_im], axis=1)
    out = np.arange(span)
    angle = phase(freq, out)
    inv_re = 2.0 * np.cos(angle) / span
    inv_re[0] = 1.0 / span
    inv_im = -2.0 * np.sin(angle) / span
    inv_im[0] = np.cos(math.pi * out) / span
    inverse = np.concatenate([inv_re, inv_im], axis=0)
    fwd = np.concatenate(high_low(forward), axis=0)
    inv = np.stack(high_low(inverse), axis=0)
    return fwd, inv


def kernel(
    n_ctx, n_ch, channels_all,
    sig_hbm, tap_hbm, gate_hbm, gain_ref, skip_ref, fwd_hbm, inv_hbm, out_ref,
    sig, tap, gate, fwd, inv, in_sem,
    outbox, inbox, send_sem, recv_sem,
    part, part_send, part_recv, power, power_send, power_recv,
    columns, normed, spec_x, spec_h, spec_y, tail,
    back_out, back_in, back_send, back_recv,
):
    rows, chans = sig.shape
    cpd = chans // n_ctx
    half = cpd // 2
    me = lax.axis_index("ctx")
    me_ch = lax.axis_index("ch")

    loads = [
        pltpu.make_async_copy(src, dst, in_sem.at[k])
        for k, (src, dst) in enumerate(
            ((sig_hbm, sig), (tap_hbm, tap), (fwd_hbm, fwd), (gate_hbm, gate), (inv_hbm, inv))
        )
    ]
    for load in loads:
        load.start()

    barrier = pltpu.get_barrier_semaphore()

    def greet_ctx(d, _):
        pl.semaphore_signal(barrier, inc=1, device_id={"ctx": lax.rem(me + d, n_ctx)}, device_id_type=MESH)
        return 0

    def greet_ch(d, _):
        pl.semaphore_signal(barrier, inc=1, device_id={"ch": lax.rem(me_ch + d, n_ch)}, device_id_type=MESH)
        return 0

    lax.fori_loop(1, n_ch, greet_ch, 0)
    lax.fori_loop(1, n_ctx, greet_ctx, 0)

    loads[0].wait()
    values = sig[...].astype(jnp.float32).T
    part[pl.ds(me_ch, 1)] = jnp.sum(values * values, axis=0, keepdims=True).reshape(1, 1, rows)
    outbox[:, 0] = values.astype(jnp.bfloat16).reshape(n_ctx, cpd, rows)
    loads[1].wait()
    outbox[:, 1] = tap[...].astype(jnp.float32).T.astype(jnp.bfloat16).reshape(n_ctx, cpd, rows)

    pl.semaphore_wait(barrier, n_ctx + n_ch - 2)

    def part_copy(peer, slot):
        return pltpu.make_async_remote_copy(
            src_ref=part.at[me_ch], dst_ref=part.at[slot], send_sem=part_send.at[peer], recv_sem=part_recv.at[slot],
            device_id={"ch": peer}, device_id_type=MESH,
        )

    def bulk_copy(peer, slot):
        return pltpu.make_async_remote_copy(
            src_ref=outbox.at[peer], dst_ref=inbox.at[slot], send_sem=send_sem.at[peer], recv_sem=recv_sem.at[slot],
            device_id={"ctx": peer}, device_id_type=MESH,
        )

    def power_copy(peer, slot):
        return pltpu.make_async_remote_copy(
            src_ref=power.at[me], dst_ref=power.at[slot], send_sem=power_send.at[peer], recv_sem=power_recv.at[slot],
            device_id={"ctx": peer}, device_id_type=MESH,
        )

    def back_copy(peer, slot):
        return pltpu.make_async_remote_copy(
            src_ref=back_out.at[peer], dst_ref=back_in.at[slot], send_sem=back_send.at[peer], recv_sem=back_recv.at[slot],
            device_id={"ctx": peer}, device_id_type=MESH,
        )

    def ctx_peer(n):
        far = n_ctx // 2 - n // 2
        return lax.rem(jnp.where(n % 2 == 0, me + far, me + n_ctx - far), n_ctx)

    def over_ctx(action):
        def step(n, _):
            action(ctx_peer(n))
            return 0
        lax.fori_loop(1, n_ctx, step, 0)

    def over_ch(action):
        def step(d, _):
            action(lax.rem(me_ch + d, n_ch))
            return 0
        lax.fori_loop(1, n_ch, step, 0)

    over_ch(lambda peer: part_copy(peer, me_ch).start())
    over_ctx(lambda peer: bulk_copy(peer, me).start())
    inbox[pl.ds(me, 1)] = outbox[pl.ds(me, 1)]

    first = me * cpd
    width = columns.shape[1]
    spot = pl.ds(pl.multiple_of(lax.rem(first, width), cpd), cpd)
    for k, ref in enumerate((gain_ref, skip_ref)):
        line = ref[pl.ds(first // width, 1), :]
        columns[k] = jnp.broadcast_to(line, (rows, width)).T
    gain = columns[0, spot, :]
    skip = columns[1, spot, :]

    over_ch(lambda peer: part_copy(peer, peer).wait_recv())
    total = jnp.sum(part[...], axis=0, keepdims=True)
    power[pl.ds(me, 1)] = lax.rsqrt(total / channels_all + EPS)
    over_ctx(lambda peer: power_copy(peer, me).start())

    lane = lax.broadcasted_iota(jnp.int32, (1, 1, rows), 2)
    spec_h[:, :STEP] = jnp.zeros((3, STEP, cpd, rows), jnp.float32)
    tail[...] = jnp.zeros_like(tail)
    over_ctx(lambda peer: power_copy(peer, peer).wait_recv())
    over_ctx(lambda peer: bulk_copy(peer, peer).wait_recv())
    loads[2].wait()

    def transform(n, _):
        at = pl.ds(pl.multiple_of(n * STEP, STEP), STEP)
        later = pl.ds(pl.multiple_of(n * STEP + STEP, STEP), STEP)
        features = inbox[at, 0].astype(jnp.float32)
        scaled = (features * power[at] * gain[None]).astype(jnp.bfloat16)
        normed[at] = scaled
        both = jnp.concatenate([scaled, inbox[at, 1]], axis=0).reshape(2 * STEP * cpd, rows)
        spectrum = jnp.dot(
            jnp.concatenate([both, both], axis=1), fwd[...], preferred_element_type=jnp.float32
        ).reshape(2, STEP, cpd, 2 * rows)
        spec_x[0, at] = spectrum[0, :, :, :rows]
        spec_x[1, at] = spectrum[0, :, :, rows:]
        h_re = spectrum[1, :, :, :rows]
        h_im = spectrum[1, :, :, rows:]
        spec_h[0, later] = h_re
        spec_h[1, later] = jnp.where(lane == 0, 0.0, h_im)
        spec_h[2, later] = jnp.where(lane == 0, h_im, h_re)
        return 0

    lax.fori_loop(0, n_ctx // STEP, transform, 0)

    def convolve(n, _):
        for part_no in range(2):
            sub = pl.ds(part_no * half, half)

            def add_blocks(m, sums):
                sums = list(sums)
                base = (n - m) * STEP
                for b in range(STEP):
                    x_re = spec_x[0, m * STEP + b, sub, :]
                    x_im = spec_x[1, m * STEP + b, sub, :]
                    for a in range(STEP):
                        k = base + a - b + STEP
                        h_re = spec_h[0, k, sub, :]
                        h_im = spec_h[1, k, sub, :]
                        h_ny = spec_h[2, k, sub, :]
                        sums[2 * a] += x_re * h_re - x_im * h_im
                        sums[2 * a + 1] += x_re * h_im + x_im * h_ny
                return tuple(sums)

            blank = jnp.zeros((half, rows), jnp.float32)
            sums = lax.fori_loop(0, n + 1, add_blocks, (blank,) * (2 * STEP))
            for a in range(STEP):
                spec_y[n * STEP + a, sub, :rows] = sums[2 * a]
                spec_y[n * STEP + a, sub, rows:] = sums[2 * a + 1]
        return 0

    lax.fori_loop(0, n_ctx // STEP, convolve, 0)
    loads[4].wait()

    def restore(n, _):
        at = pl.ds(pl.multiple_of(n * STEP, STEP), STEP)
        wave = spec_y[at].reshape(STEP * cpd, 2 * rows)
        high = wave.astype(jnp.bfloat16)
        low = (wave - high.astype(jnp.float32)).astype(jnp.bfloat16)
        time = (
            jnp.dot(high, inv[0], preferred_element_type=jnp.float32)
            + jnp.dot(low, inv[0], preferred_element_type=jnp.float32)
            + jnp.dot(high, inv[1], preferred_element_type=jnp.float32)
        ).reshape(STEP, cpd, 2 * rows)
        late = time[:, :, rows:]
        before = jnp.concatenate([tail[...], late[: STEP - 1]], axis=0)
        tail[...] = late[STEP - 1 :]
        direct = skip[None] * normed[at].astype(jnp.float32)
        back_out[at] = (time[:, :, :rows] + before + direct).astype(jnp.bfloat16)
        return 0

    lax.fori_loop(0, n_ctx // STEP, restore, 0)
    over_ctx(lambda peer: back_copy(peer, me).start())
    back_in[pl.ds(me, 1)] = back_out[pl.ds(me, 1)]
    loads[3].wait()
    over_ctx(lambda peer: back_copy(peer, peer).wait_recv())
    result = back_in[...].reshape(chans, rows).astype(jnp.float32).T
    out_ref[...] = (gate[...].astype(jnp.float32) * result).astype(jnp.bfloat16)

    over_ch(lambda peer: part_copy(peer, me_ch).wait_send())
    over_ctx(lambda peer: bulk_copy(peer, me).wait_send())
    over_ctx(lambda peer: power_copy(peer, me).wait_send())
    over_ctx(lambda peer: back_copy(peer, me).wait_send())


def solution(mesh):
    n_ctx, n_ch = mesh.shape["ctx"], mesh.shape["ch"]

    def local(signal, norm_gain, skip_gain, filter_taps, out_gate):
        rows, chans = signal.shape
        cpd = chans // n_ctx
        fwd, inv = (jnp.asarray(table) for table in dft_tables(rows))
        f32, bf16 = jnp.float32, jnp.bfloat16
        vmem, dma = pltpu.VMEM, pltpu.SemaphoreType.DMA
        anywhere = pl.BlockSpec(memory_space=pltpu.HBM)
        in_vmem = pl.BlockSpec(memory_space=pltpu.VMEM)
        return pl.pallas_call(
            functools.partial(kernel, n_ctx, n_ch, chans * n_ch),
            out_shape=jax.ShapeDtypeStruct((rows, chans), bf16),
            in_specs=[anywhere] * 3 + [in_vmem] * 2 + [anywhere] * 2,
            out_specs=in_vmem,
            scratch_shapes=[
                vmem((rows, chans), bf16), vmem((rows, chans), bf16), vmem((rows, chans), bf16),
                vmem((2 * rows, 2 * rows), bf16), vmem((2, 2 * rows, 2 * rows), bf16), dma((5,)),
                vmem((n_ctx, 2, cpd, rows), bf16), vmem((n_ctx, 2, cpd, rows), bf16), dma((n_ctx,)), dma((n_ctx,)),
                vmem((n_ch, 1, rows), f32), dma((n_ch,)), dma((n_ch,)),
                vmem((n_ctx, 1, rows), f32), dma((n_ctx,)), dma((n_ctx,)),
                vmem((2, 128, rows), f32), vmem((n_ctx, cpd, rows), bf16),
                vmem((2, n_ctx, cpd, rows), f32), vmem((3, n_ctx + STEP, cpd, rows), f32),
                vmem((n_ctx, cpd, 2 * rows), f32), vmem((1, cpd, rows), f32),
                vmem((n_ctx, cpd, rows), bf16), vmem((n_ctx, cpd, rows), bf16), dma((n_ctx,)), dma((n_ctx,)),
            ],
            compiler_params=pltpu.CompilerParams(
                collective_id=0, has_side_effects=True, vmem_limit_bytes=62 * 1024 * 1024
            ),
        )(signal, filter_taps, out_gate, norm_gain.reshape(-1, 128), skip_gain.reshape(-1, 128), fwd, inv)

    return jax.shard_map(
        local,
        mesh=mesh,
        in_specs=(P("ctx", "ch"), P("ch"), P("ch"), P("ctx", "ch"), P("ctx", "ch")),
        out_specs=P("ctx", "ch"),
        check_vma=False,
    )
```

```python
import functools
import math

import jax
import jax.numpy as jnp
import ml_dtypes
import numpy as np
from jax import lax
from jax.experimental import pallas as pl
from jax.experimental.pallas import tpu as pltpu
from jax.sharding import PartitionSpec as P

C = 8192
EPS = 1e-06
MESH = pl.DeviceIdType.MESH
STEP = 4


def high_low(table):
    high = table.astype(ml_dtypes.bfloat16)
    low = (table - high.astype(np.float64)).astype(ml_dtypes.bfloat16)
    return high, low


def dft_tables(rows):
    span = 2 * rows
    freq = np.arange(rows)

    def phase(a, b):
        return (a[:, None] * b[None, :] % span) * (2.0 * math.pi / span)

    row = np.arange(rows)
    angle = phase(row, freq)
    fwd_im = -np.sin(angle)
    fwd_im[:, 0] = np.cos(math.pi * row)
    forward = np.concatenate([np.cos(angle), fwd_im], axis=1)
    out = np.arange(span)
    angle = phase(freq, out)
    inv_re = 2.0 * np.cos(angle) / span
    inv_re[0] = 1.0 / span
    inv_im = -2.0 * np.sin(angle) / span
    inv_im[0] = np.cos(math.pi * out) / span
    high, low = high_low(np.concatenate([inv_re, inv_im], axis=0))
    return np.concatenate(high_low(forward), axis=0), np.concatenate([high, high, low], axis=0)


def kernel(
    n_ctx, n_ch, channels_all,
    sig_hbm, tap_hbm, gate_hbm, gain_hbm, skip_hbm, fwd_hbm, inv_hbm, out_ref,
    sig, tap, gate, gain, skip, fwd, inv, load_sem,
    part, part_send, part_recv,
    tap_out, tap_in, x_out, x_in, back_out, back_in, send_sem, recv_sem,
    normed, spec_x, spec_h, spec_y,
):
    rows, chans = sig.shape
    cpd = chans // n_ctx
    half = cpd // 2
    me = lax.axis_index("ctx")
    me_ch = lax.axis_index("ch")

    loads = [
        pltpu.make_async_copy(src, dst, load_sem.at[k])
        for k, (src, dst) in enumerate(
            (
                (sig_hbm, sig), (tap_hbm, tap), (gain_hbm, gain), (fwd_hbm, fwd),
                (inv_hbm, inv), (gate_hbm, gate), (skip_hbm, skip),
            )
        )
    ]
    for load in loads:
        load.start()

    barrier = pltpu.get_barrier_semaphore()

    def ctx_peer(n):
        far = n_ctx // 2 - n // 2
        return lax.rem(jnp.where(n % 2 == 0, me + far, me + n_ctx - far), n_ctx)

    def over_ctx(action):
        def step(n, _):
            action(ctx_peer(n))
            return 0

        lax.fori_loop(1, n_ctx, step, 0)

    def over_ch(action):
        def step(d, _):
            action(lax.rem(me_ch + d, n_ch))
            return 0

        lax.fori_loop(1, n_ch, step, 0)

    def part_copy(peer, slot):
        return pltpu.make_async_remote_copy(
            src_ref=part.at[me_ch], dst_ref=part.at[slot], send_sem=part_send.at[peer], recv_sem=part_recv.at[slot],
            device_id={"ch": peer}, device_id_type=MESH,
        )

    def tile_copy(source, target, k, peer):
        return pltpu.make_async_remote_copy(
            src_ref=source.at[peer], dst_ref=target.at[me], send_sem=send_sem.at[k], recv_sem=recv_sem.at[k],
            device_id={"ctx": peer}, device_id_type=MESH,
        )

    def all_tiles(source, target, k):
        return pltpu.make_async_remote_copy(
            src_ref=source.at[pl.ds(0, n_ctx - 1)], dst_ref=target.at[pl.ds(0, n_ctx - 1)],
            send_sem=send_sem.at[k], recv_sem=recv_sem.at[k],
            device_id={"ctx": ctx_peer(1)}, device_id_type=MESH,
        )

    over_ctx(lambda peer: pl.semaphore_signal(barrier, inc=1, device_id={"ctx": peer}, device_id_type=MESH))
    over_ch(lambda peer: pl.semaphore_signal(barrier, inc=1, device_id={"ch": peer}, device_id_type=MESH))

    loads[0].wait()
    values = sig[...].astype(jnp.float32)
    squares = values * values
    lanes = squares[:, :128]
    for k in range(1, chans // 128):
        lanes += squares[:, k * 128 : (k + 1) * 128]
    part[pl.ds(me_ch, 1)] = jnp.sum(lanes.T, axis=0, keepdims=True).reshape(1, 1, rows)
    loads[1].wait()
    tap_out[...] = tap[...].astype(jnp.float32).T.astype(jnp.bfloat16).reshape(n_ctx, cpd, rows)

    pl.semaphore_wait(barrier, n_ctx + n_ch - 2)
    over_ch(lambda peer: part_copy(peer, me_ch).start())
    over_ctx(lambda peer: tile_copy(tap_out, tap_in, 0, peer).start())
    tap_in[pl.ds(me, 1)] = tap_out[pl.ds(me, 1)]

    loads[2].wait()
    over_ch(lambda peer: part_copy(peer, peer).wait_recv())
    total = jnp.sum(part[...], axis=0)
    scale = jnp.broadcast_to(lax.rsqrt(total / channels_all + EPS), (128, rows)).T
    for k in range(chans // 128):
        at = pl.ds(k * 128, 128)
        normed[:, at] = (sig[:, at].astype(jnp.float32) * scale * gain[:, at]).astype(jnp.bfloat16)
    x_out[...] = normed[...].astype(jnp.float32).T.astype(jnp.bfloat16).reshape(n_ctx, cpd, rows)
    over_ctx(lambda peer: tile_copy(x_out, x_in, 1, peer).start())
    x_in[pl.ds(me, 1)] = x_out[pl.ds(me, 1)]

    def spectrum(tiles):
        lines = tiles.reshape(n_ctx * cpd, rows)
        both = jnp.concatenate([lines, lines], axis=1)
        return jnp.dot(both, fwd[...], preferred_element_type=jnp.float32).reshape(n_ctx, cpd, 2 * rows)

    lane = lax.broadcasted_iota(jnp.int32, (1, 1, rows), 2)
    spec_h[:, :STEP] = jnp.zeros((3, STEP, cpd, rows), jnp.float32)
    loads[3].wait()
    all_tiles(tap_out, tap_in, 0).wait_recv()
    filters = spectrum(tap_in[...])
    h_re, h_im = filters[:, :, :rows], filters[:, :, rows:]
    spec_h[0, STEP:] = h_re
    spec_h[1, STEP:] = jnp.where(lane == 0, 0.0, h_im)
    spec_h[2, STEP:] = jnp.where(lane == 0, h_im, h_re)

    all_tiles(x_out, x_in, 1).wait_recv()
    features = spectrum(x_in[...])
    spec_x[0] = features[:, :, :rows]
    spec_x[1] = features[:, :, rows:]

    def convolve(n, _):
        for part_no in range(2):
            sub = pl.ds(part_no * half, half)

            def add_blocks(m, sums):
                sums = list(sums)
                base = (n - m) * STEP
                for b in range(STEP):
                    x_re = spec_x[0, m * STEP + b, sub, :]
                    x_im = spec_x[1, m * STEP + b, sub, :]
                    for a in range(STEP):
                        k = base + a - b + STEP
                        h_re = spec_h[0, k, sub, :]
                        h_im = spec_h[1, k, sub, :]
                        h_ny = spec_h[2, k, sub, :]
                        sums[2 * a] += x_re * h_re - x_im * h_im
                        sums[2 * a + 1] += x_re * h_im + x_im * h_ny
                return tuple(sums)

            blank = jnp.zeros((half, rows), jnp.float32)
            sums = lax.fori_loop(0, n + 1, add_blocks, (blank,) * (2 * STEP))
            for a in range(STEP):
                spec_y[n * STEP + a, sub, :rows] = sums[2 * a]
                spec_y[n * STEP + a, sub, rows:] = sums[2 * a + 1]
        return 0

    lax.fori_loop(0, n_ctx // STEP, convolve, 0)

    loads[4].wait()
    wave = spec_y[...].reshape(n_ctx * cpd, 2 * rows)
    high = wave.astype(jnp.bfloat16)
    low = (wave - high.astype(jnp.float32)).astype(jnp.bfloat16)
    time = jnp.dot(
        jnp.concatenate([high, low, high], axis=1), inv[...], preferred_element_type=jnp.float32
    ).reshape(n_ctx, cpd, 2 * rows)
    early, late = time[:, :, :rows], time[:, :, rows:]
    back_out[...] = (
        early + jnp.concatenate([jnp.zeros((1, cpd, rows), jnp.float32), late[: n_ctx - 1]], axis=0)
    ).astype(jnp.bfloat16)

    over_ctx(lambda peer: tile_copy(back_out, back_in, 2, peer).start())
    back_in[pl.ds(me, 1)] = back_out[pl.ds(me, 1)]
    loads[5].wait()
    loads[6].wait()
    all_tiles(back_out, back_in, 2).wait_recv()
    result = back_in[...].reshape(chans, rows).astype(jnp.float32).T
    direct = skip[...] * normed[...].astype(jnp.float32)
    out_ref[...] = (gate[...].astype(jnp.float32) * (result + direct)).astype(jnp.bfloat16)

    over_ch(lambda peer: part_copy(peer, me_ch).wait_send())
    all_tiles(tap_out, tap_in, 0).wait_send()
    all_tiles(x_out, x_in, 1).wait_send()
    all_tiles(back_out, back_in, 2).wait_send()


def solution(mesh):
    n_ctx, n_ch = mesh.shape["ctx"], mesh.shape["ch"]

    def local(signal, norm_gain, skip_gain, filter_taps, out_gate):
        rows, chans = signal.shape
        cpd = chans // n_ctx
        fwd, inv = (jnp.asarray(table) for table in dft_tables(rows))
        f32, bf16 = jnp.float32, jnp.bfloat16
        vmem, dma = pltpu.VMEM, pltpu.SemaphoreType.DMA
        hbm = pl.BlockSpec(memory_space=pltpu.HBM)
        block, tiles = vmem((rows, chans), bf16), vmem((n_ctx, cpd, rows), bf16)
        return pl.pallas_call(
            functools.partial(kernel, n_ctx, n_ch, chans * n_ch),
            out_shape=jax.ShapeDtypeStruct((rows, chans), bf16),
            in_specs=[hbm] * 7,
            out_specs=pl.BlockSpec(memory_space=pltpu.VMEM),
            scratch_shapes=[
                block, block, block, vmem((1, chans), f32), vmem((1, chans), f32),
                vmem(fwd.shape, bf16), vmem(inv.shape, bf16), dma((7,)),
                vmem((n_ch, 1, rows), f32), dma((n_ch,)), dma((n_ch,)),
                tiles, tiles, tiles, tiles, tiles, tiles, dma((3,)), dma((3,)),
                block, vmem((2, n_ctx, cpd, rows), f32), vmem((3, n_ctx + STEP, cpd, rows), f32),
                vmem((n_ctx, cpd, 2 * rows), f32),
            ],
            compiler_params=pltpu.CompilerParams(
                collective_id=0, has_side_effects=True, vmem_limit_bytes=62 * 1024 * 1024
            ),
        )(signal, filter_taps, out_gate, norm_gain.reshape(1, -1), skip_gain.reshape(1, -1), fwd, inv)

    return jax.shard_map(
        local,
        mesh=mesh,
        in_specs=(P("ctx", "ch"), P("ch"), P("ch"), P("ctx", "ch"), P("ctx", "ch")),
        out_specs=P("ctx", "ch"),
        check_vma=False,
    )
```

```python
import functools
import math

import jax
import jax.numpy as jnp
import ml_dtypes
import numpy as np
from jax import lax
from jax.experimental import pallas as pl
from jax.experimental.pallas import tpu as pltpu
from jax.sharding import PartitionSpec as P

C = 8192
EPS = 1e-06
MESH = pl.DeviceIdType.MESH
STEP = 4


def high_low(table):
    high = table.astype(ml_dtypes.bfloat16)
    low = (table - high.astype(np.float64)).astype(ml_dtypes.bfloat16)
    return high, low


def dft_tables(rows):
    span = 2 * rows
    freq = np.arange(rows)

    def phase(a, b):
        return (a[:, None] * b[None, :] % span) * (2.0 * math.pi / span)

    row = np.arange(rows)
    angle = phase(row, freq)
    fwd_im = -np.sin(angle)
    fwd_im[:, 0] = np.cos(math.pi * row)
    forward = np.concatenate([np.cos(angle), fwd_im], axis=1)
    out = np.arange(span)
    angle = phase(freq, out)
    inv_re = 2.0 * np.cos(angle) / span
    inv_re[0] = 1.0 / span
    inv_im = -2.0 * np.sin(angle) / span
    inv_im[0] = np.cos(math.pi * out) / span
    high, low = high_low(np.concatenate([inv_re, inv_im], axis=0))
    return np.concatenate(high_low(forward), axis=0), np.concatenate([high, high, low], axis=0)


def kernel(
    n_ctx, n_ch, channels_all,
    sig_hbm, tap_hbm, gate_hbm, gain_hbm, skip_hbm, fwd_hbm, inv_hbm, out_ref,
    sig, tap, gate, gain, skip, fwd, inv, load_sem,
    part, part_send, part_recv,
    tap_out, tap_relay, tap_in, x_out, x_in, back_out, back_in,
    send_sem, recv_sem, relay_send, relay_recv, pass_send, far_sem,
    normed, spec_x, spec_h, spec_y,
):
    rows, chans = sig.shape
    cpd = chans // n_ctx
    me = lax.axis_index("ctx")
    me_ch = lax.axis_index("ch")
    chip, core, n_chips = me // 2, lax.rem(me, 2), n_ctx // 2
    reach, turn = n_chips // 4, n_chips // 2
    relayed = 2 * (turn - reach) - 1

    loads = [
        pltpu.make_async_copy(src, dst, load_sem.at[k])
        for k, (src, dst) in enumerate(
            (
                (sig_hbm, sig), (tap_hbm, tap), (gain_hbm, gain), (fwd_hbm, fwd),
                (inv_hbm, inv), (gate_hbm, gate), (skip_hbm, skip),
            )
        )
    ]

    barrier = pltpu.get_barrier_semaphore()

    def chip_away(far, right):
        return lax.rem(jnp.where(right, chip + far, chip + n_chips - far), n_chips)

    def over_ctx(action):
        def step(n, _):
            q = n // 2
            peer_chip = chip_away(turn - (q + 1) // 2, q % 2 == 1)
            action(2 * peer_chip + jnp.where(n < n_ctx - 2, n % 2, 1 - core))
            return 0

        lax.fori_loop(0, n_ctx - 1, step, 0)

    def over_near(action):
        def step(n, _):
            peer_chip = chip_away(reach - n // 4, (n // 2) % 2 == 1)
            action(2 * peer_chip + jnp.where(n < 4 * reach, n % 2, 1 - core))
            return 0

        lax.fori_loop(0, 4 * reach + 1, step, 0)

    def over_ch(action):
        def step(d, _):
            action(lax.rem(me_ch + d, n_ch))
            return 0

        lax.fori_loop(1, n_ch, step, 0)

    def part_copy(peer, slot):
        return pltpu.make_async_remote_copy(
            src_ref=part.at[me_ch], dst_ref=part.at[slot], send_sem=part_send.at[peer], recv_sem=part_recv.at[slot],
            device_id={"ch": peer}, device_id_type=MESH,
        )

    def tile_copy(source, target, k, peer):
        return pltpu.make_async_remote_copy(
            src_ref=source.at[peer], dst_ref=target.at[me], send_sem=send_sem.at[k], recv_sem=recv_sem.at[k],
            device_id={"ctx": peer}, device_id_type=MESH,
        )

    def tiles_of(target, count, k):
        return pltpu.make_async_remote_copy(
            src_ref=target.at[pl.ds(0, count)], dst_ref=target.at[pl.ds(0, count)],
            send_sem=send_sem.at[k], recv_sem=recv_sem.at[k],
            device_id={"ctx": lax.rem(me + 1, n_ctx)}, device_id_type=MESH,
        )

    def relay_copy(source, relay, k, side):
        far_first = 2 * chip_away(reach + 1, True) if side == 0 else 2 * chip_away(turn, False) + 1
        return pltpu.make_async_remote_copy(
            src_ref=source.at[pl.ds(far_first, relayed)], dst_ref=relay.at[side],
            send_sem=relay_send.at[side], recv_sem=relay_recv.at[side],
            device_id={"ctx": 2 * chip_away(reach, side == 0) + core}, device_id_type=MESH,
        )

    def pass_on(relay, target, k, side, action):
        origin = 2 * chip_away(reach, side == 1) + core
        far_first = 2 * (chip + 1) if side == 0 else 2 * (chip + n_chips + reach - turn) + 1

        def step(t, _):
            action(
                pltpu.make_async_remote_copy(
                    src_ref=relay.at[side, t], dst_ref=target.at[origin],
                    send_sem=pass_send, recv_sem=recv_sem.at[k],
                    device_id={"ctx": lax.rem(far_first + t, n_ctx)}, device_id_type=MESH,
                )
            )
            return 0

        lax.fori_loop(0, relayed, step, 0)

    def send_tiles(source, relay, target, k):
        for side in range(2):
            relay_copy(source, relay, k, side).start()
        over_near(lambda peer: tile_copy(source, target, k, peer).start())
        target[pl.ds(me, 1)] = source[pl.ds(me, 1)]

    def forward_tiles(source, relay, target, k):
        for side in range(2):
            relay_copy(source, relay, k, side).wait_recv()
            pass_on(relay, target, k, side, lambda copy: copy.start())

    over_near(lambda peer: pl.semaphore_signal(barrier, inc=1, device_id={"ctx": peer}, device_id_type=MESH))
    over_ch(lambda peer: pl.semaphore_signal(barrier, inc=1, device_id={"ch": peer}, device_id_type=MESH))
    for load in loads:
        load.start()

    loads[0].wait()
    values = sig[...].astype(jnp.float32)
    squares = values * values
    lanes = squares[:, :128]
    for k in range(1, chans // 128):
        lanes += squares[:, k * 128 : (k + 1) * 128]
    part[pl.ds(me_ch, 1)] = jnp.sum(lanes.T, axis=0, keepdims=True).reshape(1, 1, rows)
    loads[1].wait()
    tap_tiles = tap[...].astype(jnp.float32).T.astype(jnp.bfloat16).reshape(n_ctx, cpd, rows)
    tap_out[:n_ctx] = tap_tiles
    tap_out[n_ctx:] = tap_tiles

    pl.semaphore_wait(barrier, 4 * reach + 1 + n_ch - 1)
    for right in (True, False):
        pl.semaphore_signal(
            far_sem, inc=1, device_id={"ctx": 2 * chip_away(reach, right) + core}, device_id_type=MESH
        )
    over_ch(lambda peer: part_copy(peer, me_ch).start())
    send_tiles(tap_out, tap_relay, tap_in, 0)

    loads[2].wait()
    over_ch(lambda peer: part_copy(peer, peer).wait_recv())
    total = jnp.sum(part[...], axis=0)
    scale = jnp.broadcast_to(lax.rsqrt(total / channels_all + EPS), (128, rows)).T
    for k in range(chans // 128):
        at = pl.ds(k * 128, 128)
        normed[:, at] = (sig[:, at].astype(jnp.float32) * scale * gain[:, at]).astype(jnp.bfloat16)
    x_tiles = normed[...].astype(jnp.float32).T.astype(jnp.bfloat16).reshape(n_ctx, cpd, rows)
    x_out[...] = x_tiles
    pl.semaphore_wait(far_sem, 2)
    over_ctx(lambda peer: tile_copy(x_out, x_in, 1, peer).start())
    x_in[pl.ds(me, 1)] = x_out[pl.ds(me, 1)]
    forward_tiles(tap_out, tap_relay, tap_in, 0)

    def spectrum(tiles):
        lines = tiles.reshape(n_ctx * cpd, rows)
        both = jnp.concatenate([lines, lines], axis=1)
        return jnp.dot(both, fwd[...], preferred_element_type=jnp.float32).reshape(n_ctx, cpd, 2 * rows)

    spec_h[:, :STEP] = jnp.zeros((3, STEP, cpd, rows), jnp.float32)
    loads[3].wait()

    def keep_spectrum(tiles, spec, first):
        whole = spectrum(tiles)
        re, im = whole[:, :, :rows], whole[:, :, rows:]
        spec[0, first:] = re
        spec[1, first:] = im
        spec[2, first:] = re + im

    tiles_of(tap_in, n_ctx - 1, 0).wait_recv()
    keep_spectrum(tap_in[...], spec_h, STEP)
    tiles_of(x_in, n_ctx - 1, 1).wait_recv()
    keep_spectrum(x_in[...], spec_x, 0)

    lane = lax.broadcasted_iota(jnp.int32, (cpd, rows), 1)

    def convolve(n, _):
        def add_blocks(m, sums):
            sums = list(sums)
            base = (n - m) * STEP
            for b in range(STEP):
                x = [spec_x[k, m * STEP + b] for k in range(3)]
                for a in range(STEP):
                    for k in range(3):
                        sums[3 * a + k] += x[k] * spec_h[k, base + a - b + STEP]
            return tuple(sums)

        blank = jnp.zeros((cpd, rows), jnp.float32)
        sums = lax.fori_loop(0, n + 1, add_blocks, (blank,) * (3 * STEP))
        for a in range(STEP):
            re, im, both = sums[3 * a : 3 * a + 3]
            spec_y[n * STEP + a, :, :rows] = jnp.where(lane == 0, re, re - im)
            spec_y[n * STEP + a, :, rows:] = jnp.where(lane == 0, im, both - re - im)
        return 0

    lax.fori_loop(0, n_ctx // STEP, convolve, 0)

    loads[4].wait()
    wave = spec_y[...].reshape(n_ctx * cpd, 2 * rows)
    high = wave.astype(jnp.bfloat16)
    low = (wave - high.astype(jnp.float32)).astype(jnp.bfloat16)
    time = jnp.dot(
        jnp.concatenate([high, low, high], axis=1), inv[...], preferred_element_type=jnp.float32
    ).reshape(n_ctx, cpd, 2 * rows)
    early, late = time[:, :, :rows], time[:, :, rows:]
    back_out[...] = (
        early + jnp.concatenate([jnp.zeros((1, cpd, rows), jnp.float32), late[: n_ctx - 1]], axis=0)
    ).astype(jnp.bfloat16)

    over_ctx(lambda peer: tile_copy(back_out, back_in, 2, peer).start())
    back_in[pl.ds(me, 1)] = back_out[pl.ds(me, 1)]
    loads[5].wait()
    loads[6].wait()
    direct = skip[...] * normed[...].astype(jnp.float32)
    tiles_of(back_in, n_ctx - 1, 2).wait_recv()
    result = back_in[...].reshape(chans, rows).astype(jnp.float32).T
    out_ref[...] = (gate[...].astype(jnp.float32) * (result + direct)).astype(jnp.bfloat16)

    over_ch(lambda peer: part_copy(peer, me_ch).wait_send())
    tiles_of(tap_in, 4 * reach + 1, 0).wait_send()
    for side in range(2):
        relay_copy(tap_out, tap_relay, 0, side).wait_send()
        pass_on(tap_relay, tap_in, 0, side, lambda copy: copy.wait_send())
    tiles_of(x_in, n_ctx - 1, 1).wait_send()
    tiles_of(back_in, n_ctx - 1, 2).wait_send()


def solution(mesh):
    n_ctx, n_ch = mesh.shape["ctx"], mesh.shape["ch"]

    def local(signal, norm_gain, skip_gain, filter_taps, out_gate):
        rows, chans = signal.shape
        cpd = chans // n_ctx
        fwd, inv = (jnp.asarray(table) for table in dft_tables(rows))
        f32, bf16 = jnp.float32, jnp.bfloat16
        vmem, dma = pltpu.VMEM, pltpu.SemaphoreType.DMA
        hbm = pl.BlockSpec(memory_space=pltpu.HBM)
        block, tiles = vmem((rows, chans), bf16), vmem((n_ctx, cpd, rows), bf16)
        twice = vmem((2 * n_ctx, cpd, rows), bf16)
        relay = vmem((2, 2 * (n_ctx // 4 - n_ctx // 8) - 1, cpd, rows), bf16)
        return pl.pallas_call(
            functools.partial(kernel, n_ctx, n_ch, chans * n_ch),
            out_shape=jax.ShapeDtypeStruct((rows, chans), bf16),
            in_specs=[hbm] * 7,
            out_specs=pl.BlockSpec(memory_space=pltpu.VMEM),
            scratch_shapes=[
                block, block, block, vmem((1, chans), f32), vmem((1, chans), f32),
                vmem(fwd.shape, bf16), vmem(inv.shape, bf16), dma((7,)),
                vmem((n_ch, 1, rows), f32), dma((n_ch,)), dma((n_ch,)),
                twice, relay, tiles, tiles, tiles, tiles, tiles,
                dma((3,)), dma((3,)), dma((2,)), dma((2,)), dma(()), pltpu.SemaphoreType.REGULAR,
                block, vmem((3, n_ctx, cpd, rows), f32), vmem((3, n_ctx + STEP, cpd, rows), f32),
                vmem((n_ctx, cpd, 2 * rows), f32),
            ],
            compiler_params=pltpu.CompilerParams(
                collective_id=0, has_side_effects=True, vmem_limit_bytes=62 * 1024 * 1024
            ),
        )(signal, filter_taps, out_gate, norm_gain.reshape(1, -1), skip_gain.reshape(1, -1), fwd, inv)

    return jax.shard_map(
        local,
        mesh=mesh,
        in_specs=(P("ctx", "ch"), P("ch"), P("ch"), P("ctx", "ch"), P("ctx", "ch")),
        out_specs=P("ctx", "ch"),
        check_vma=False,
    )
```

```python
import functools
import math

import jax
import jax.numpy as jnp
import ml_dtypes
import numpy as np
from jax import lax
from jax.experimental import pallas as pl
from jax.experimental.pallas import tpu as pltpu
from jax.sharding import PartitionSpec as P

C = 8192
EPS = 1e-06
MESH = pl.DeviceIdType.MESH
STEP = 8


def high_low(table):
    high = table.astype(ml_dtypes.bfloat16)
    low = (table - high.astype(np.float64)).astype(ml_dtypes.bfloat16)
    return high, low


def dft_tables(rows):
    span = 2 * rows
    freq = np.arange(rows)

    def phase(a, b):
        return (a[:, None] * b[None, :] % span) * (2.0 * math.pi / span)

    row = np.arange(rows)
    angle = phase(row, freq)
    fwd_im = -np.sin(angle)
    fwd_im[:, 0] = np.cos(math.pi * row)
    forward = np.concatenate([np.cos(angle), fwd_im], axis=1)
    out = np.arange(span)
    angle = phase(freq, out)
    inv_re = 2.0 * np.cos(angle) / span
    inv_re[0] = 1.0 / span
    inv_im = -2.0 * np.sin(angle) / span
    inv_im[0] = np.cos(math.pi * out) / span
    high, low = high_low(np.concatenate([inv_re, inv_im], axis=0))
    return np.concatenate(high_low(forward), axis=0), np.concatenate([high, high, low], axis=0)


def kernel(
    n_ctx, n_ch, channels_all,
    sig_hbm, tap_hbm, gate_hbm, gain_hbm, skip_hbm, fwd_hbm, inv_hbm, out_ref,
    sig, tap, gate, gain, skip, fwd, inv, load_sem,
    part, part_send, part_recv,
    tap_out, tap_relay, tap_in, x_out, x_in, back_out, back_in,
    send_sem, recv_sem, relay_send, relay_recv, pass_send, far_sem,
    normed, spec_x, spec_h, spec_y,
):
    rows, chans = sig.shape
    cpd = chans // n_ctx
    half = cpd // 2
    me = lax.axis_index("ctx")
    me_ch = lax.axis_index("ch")
    chip, core, n_chips = me // 2, lax.rem(me, 2), n_ctx // 2
    reach, turn = n_chips // 4, n_chips // 2
    relayed = 2 * (turn - reach) - 1

    loads = [
        pltpu.make_async_copy(src, dst, load_sem.at[k])
        for k, (src, dst) in enumerate(
            (
                (sig_hbm, sig), (tap_hbm, tap), (gain_hbm, gain), (fwd_hbm, fwd),
                (inv_hbm, inv), (gate_hbm, gate), (skip_hbm, skip),
            )
        )
    ]

    barrier = pltpu.get_barrier_semaphore()

    def chip_away(far, right):
        return lax.rem(jnp.where(right, chip + far, chip + n_chips - far), n_chips)

    def over_ctx(action):
        def step(n, _):
            q = n // 2
            peer_chip = chip_away(turn - (q + 1) // 2, q % 2 == 1)
            action(2 * peer_chip + jnp.where(n < n_ctx - 2, n % 2, 1 - core))
            return 0

        lax.fori_loop(0, n_ctx - 1, step, 0)

    def over_near(action):
        def step(n, _):
            peer_chip = chip_away(reach - n // 4, (n // 2) % 2 == 1)
            action(2 * peer_chip + jnp.where(n < 4 * reach, n % 2, 1 - core))
            return 0

        lax.fori_loop(0, 4 * reach + 1, step, 0)

    def over_ch(action):
        def step(d, _):
            action(lax.rem(me_ch + d, n_ch))
            return 0

        lax.fori_loop(1, n_ch, step, 0)

    def part_copy(peer, slot):
        return pltpu.make_async_remote_copy(
            src_ref=part.at[me_ch], dst_ref=part.at[slot], send_sem=part_send.at[peer], recv_sem=part_recv.at[slot],
            device_id={"ch": peer}, device_id_type=MESH,
        )

    def tile_copy(source, target, k, peer):
        return pltpu.make_async_remote_copy(
            src_ref=source.at[peer], dst_ref=target.at[me], send_sem=send_sem.at[k], recv_sem=recv_sem.at[k],
            device_id={"ctx": peer}, device_id_type=MESH,
        )

    def half_copy(source, target, k, peer):
        return pltpu.make_async_remote_copy(
            src_ref=source, dst_ref=target, send_sem=send_sem.at[k], recv_sem=recv_sem.at[k],
            device_id={"ctx": peer}, device_id_type=MESH,
        )

    def halves_of(source, target, k):
        return half_copy(source, target, k, lax.rem(me + 1, n_ctx))

    def tiles_of(target, count, k):
        return pltpu.make_async_remote_copy(
            src_ref=target.at[pl.ds(0, count)], dst_ref=target.at[pl.ds(0, count)],
            send_sem=send_sem.at[k], recv_sem=recv_sem.at[k],
            device_id={"ctx": lax.rem(me + 1, n_ctx)}, device_id_type=MESH,
        )

    def relay_copy(source, relay, k, side):
        far_first = 2 * chip_away(reach + 1, True) if side == 0 else 2 * chip_away(turn, False) + 1
        return pltpu.make_async_remote_copy(
            src_ref=source.at[pl.ds(far_first, relayed)], dst_ref=relay.at[side],
            send_sem=relay_send.at[side], recv_sem=relay_recv.at[side],
            device_id={"ctx": 2 * chip_away(reach, side == 0) + core}, device_id_type=MESH,
        )

    def pass_on(relay, target, k, side, action):
        origin = 2 * chip_away(reach, side == 1) + core
        far_first = 2 * (chip + 1) if side == 0 else 2 * (chip + n_chips + reach - turn) + 1

        def step(t, _):
            action(
                pltpu.make_async_remote_copy(
                    src_ref=relay.at[side, t], dst_ref=target.at[origin],
                    send_sem=pass_send, recv_sem=recv_sem.at[k],
                    device_id={"ctx": lax.rem(far_first + t, n_ctx)}, device_id_type=MESH,
                )
            )
            return 0

        lax.fori_loop(0, relayed, step, 0)

    def send_tiles(source, relay, target, k):
        for side in range(2):
            relay_copy(source, relay, k, side).start()
        over_near(lambda peer: tile_copy(source, target, k, peer).start())
        target[pl.ds(me, 1)] = source[pl.ds(me, 1)]

    def forward_tiles(source, relay, target, k):
        for side in range(2):
            relay_copy(source, relay, k, side).wait_recv()
            pass_on(relay, target, k, side, lambda copy: copy.start())

    over_near(lambda peer: pl.semaphore_signal(barrier, inc=1, device_id={"ctx": peer}, device_id_type=MESH))
    over_ch(lambda peer: pl.semaphore_signal(barrier, inc=1, device_id={"ch": peer}, device_id_type=MESH))
    for load in loads:
        load.start()

    loads[0].wait()
    values = sig[...].astype(jnp.float32)
    squares = values * values
    lanes = squares[:, :128]
    for k in range(1, chans // 128):
        lanes += squares[:, k * 128 : (k + 1) * 128]
    part[pl.ds(me_ch, 1)] = jnp.sum(lanes.T, axis=0, keepdims=True).reshape(1, 1, rows)
    loads[1].wait()
    tap_tiles = tap[...].astype(jnp.float32).T.astype(jnp.bfloat16).reshape(n_ctx, cpd, rows)
    tap_out[:n_ctx] = tap_tiles
    tap_out[n_ctx:] = tap_tiles

    pl.semaphore_wait(barrier, 4 * reach + 1 + n_ch - 1)
    for right in (True, False):
        pl.semaphore_signal(
            far_sem, inc=1, device_id={"ctx": 2 * chip_away(reach, right) + core}, device_id_type=MESH
        )
    over_ch(lambda peer: part_copy(peer, me_ch).start())
    send_tiles(tap_out, tap_relay, tap_in, 0)

    loads[2].wait()
    over_ch(lambda peer: part_copy(peer, peer).wait_recv())
    total = jnp.sum(part[...], axis=0)
    scale = jnp.broadcast_to(lax.rsqrt(total / channels_all + EPS), (128, rows)).T
    for k in range(chans // 128):
        at = pl.ds(k * 128, 128)
        normed[:, at] = (sig[:, at].astype(jnp.float32) * scale * gain[:, at]).astype(jnp.bfloat16)
    x_tiles = normed[...].astype(jnp.float32).T.reshape(n_ctx, 2, half, rows)
    x_out[...] = x_tiles.astype(jnp.bfloat16)
    pl.semaphore_wait(far_sem, 2)
    for part_no in range(2):
        over_ctx(lambda peer: half_copy(x_out.at[peer, part_no], x_in.at[part_no, me], 1 + part_no, peer).start())
        x_in[part_no, pl.ds(me, 1)] = x_out[pl.ds(me, 1), part_no]
    forward_tiles(tap_out, tap_relay, tap_in, 0)

    def spectrum(tiles):
        lines = tiles.reshape(-1, rows)
        both = jnp.concatenate([lines, lines], axis=1)
        whole = jnp.dot(both, fwd[...], preferred_element_type=jnp.float32).reshape(n_ctx, -1, 2 * rows)
        re, im = whole[:, :, :rows], whole[:, :, rows:]
        return re, im, re + im

    spec_h[:, :STEP] = jnp.zeros((3, STEP, cpd, rows), jnp.float32)
    loads[3].wait()
    tiles_of(tap_in, n_ctx - 1, 0).wait_recv()
    for k, values in enumerate(spectrum(tap_in[...])):
        spec_h[k, STEP:] = values
    loads[4].wait()

    lane = lax.broadcasted_iota(jnp.int32, (half, rows), 1)

    for part_no in range(2):
        sub = pl.ds(part_no * half, half)
        halves_of(x_in.at[part_no, pl.ds(0, n_ctx - 1)], x_in.at[part_no, pl.ds(0, n_ctx - 1)], 1 + part_no).wait_recv()
        lines = x_in[part_no].astype(jnp.float32).reshape(n_ctx * half, rows).astype(jnp.bfloat16)
        for k, values in enumerate(spectrum(lines)):
            spec_x[k] = values

        def convolve(n, _):
            def add_blocks(m, sums):
                sums = list(sums)
                base = (n - m) * STEP
                for b in range(STEP):
                    x = [spec_x[k, m * STEP + b] for k in range(3)]
                    for a in range(STEP):
                        for k in range(3):
                            sums[3 * a + k] += x[k] * spec_h[k, base + a - b + STEP, sub, :]
                return tuple(sums)

            blank = jnp.zeros((half, rows), jnp.float32)
            sums = lax.fori_loop(0, n + 1, add_blocks, (blank,) * (3 * STEP))
            for a in range(STEP):
                re, im, both = sums[3 * a : 3 * a + 3]
                spec_y[n * STEP + a, :, :rows] = jnp.where(lane == 0, re, re - im)
                spec_y[n * STEP + a, :, rows:] = jnp.where(lane == 0, im, both - re - im)
            return 0

        lax.fori_loop(0, n_ctx // STEP, convolve, 0)
        wave = spec_y[...].reshape(n_ctx * half, 2 * rows)
        high = wave.astype(jnp.bfloat16)
        low = (wave - high.astype(jnp.float32)).astype(jnp.bfloat16)
        time = jnp.dot(
            jnp.concatenate([high, low, high], axis=1), inv[...], preferred_element_type=jnp.float32
        ).reshape(n_ctx, half, 2 * rows)
        early, late = time[:, :, :rows], time[:, :, rows:]
        back_out[part_no] = (
            early + jnp.concatenate([jnp.zeros((1, half, rows), jnp.float32), late[: n_ctx - 1]], axis=0)
        ).astype(jnp.bfloat16)
        over_ctx(lambda peer: half_copy(back_out.at[part_no, peer], back_in.at[me, part_no], 3 + part_no, peer).start())
        back_in[pl.ds(me, 1), part_no] = back_out[part_no, pl.ds(me, 1)]

    loads[5].wait()
    loads[6].wait()
    direct = skip[...] * normed[...].astype(jnp.float32)
    some_back = back_in.at[pl.ds(0, n_ctx - 1), 0]
    for part_no in range(2):
        halves_of(back_out.at[part_no, pl.ds(0, n_ctx - 1)], some_back, 3 + part_no).wait_recv()
    result = back_in[...].astype(jnp.float32).reshape(chans, rows).T
    out_ref[...] = (gate[...].astype(jnp.float32) * (result + direct)).astype(jnp.bfloat16)

    over_ch(lambda peer: part_copy(peer, me_ch).wait_send())
    tiles_of(tap_in, 4 * reach + 1, 0).wait_send()
    for side in range(2):
        relay_copy(tap_out, tap_relay, 0, side).wait_send()
        pass_on(tap_relay, tap_in, 0, side, lambda copy: copy.wait_send())
    some_x = x_in.at[0, pl.ds(0, n_ctx - 1)]
    for k in range(1, 5):
        halves_of(some_x, some_x, k).wait_send()


def solution(mesh):
    n_ctx, n_ch = mesh.shape["ctx"], mesh.shape["ch"]

    def local(signal, norm_gain, skip_gain, filter_taps, out_gate):
        rows, chans = signal.shape
        cpd = chans // n_ctx
        fwd, inv = (jnp.asarray(table) for table in dft_tables(rows))
        f32, bf16 = jnp.float32, jnp.bfloat16
        vmem, dma = pltpu.VMEM, pltpu.SemaphoreType.DMA
        hbm = pl.BlockSpec(memory_space=pltpu.HBM)
        block, tiles = vmem((rows, chans), bf16), vmem((n_ctx, cpd, rows), bf16)
        twice = vmem((2 * n_ctx, cpd, rows), bf16)
        relay = vmem((2, 2 * (n_ctx // 4 - n_ctx // 8) - 1, cpd, rows), bf16)
        return pl.pallas_call(
            functools.partial(kernel, n_ctx, n_ch, chans * n_ch),
            out_shape=jax.ShapeDtypeStruct((rows, chans), bf16),
            in_specs=[hbm] * 7,
            out_specs=pl.BlockSpec(memory_space=pltpu.VMEM),
            scratch_shapes=[
                block, block, block, vmem((1, chans), f32), vmem((1, chans), f32),
                vmem(fwd.shape, bf16), vmem(inv.shape, bf16), dma((7,)),
                vmem((n_ch, 1, rows), f32), dma((n_ch,)), dma((n_ch,)),
                twice, relay, tiles, vmem((n_ctx, 2, cpd // 2, rows), bf16), vmem((2, n_ctx, cpd // 2, rows), bf16),
                vmem((2, n_ctx, cpd // 2, rows), bf16), vmem((n_ctx, 2, cpd // 2, rows), bf16),
                dma((5,)), dma((5,)), dma((2,)), dma((2,)), dma(()), pltpu.SemaphoreType.REGULAR,
                block, vmem((3, n_ctx, cpd // 2, rows), f32), vmem((3, n_ctx + STEP, cpd, rows), f32),
                vmem((n_ctx, cpd // 2, 2 * rows), f32),
            ],
            compiler_params=pltpu.CompilerParams(
                collective_id=0, has_side_effects=True, vmem_limit_bytes=62 * 1024 * 1024
            ),
        )(signal, filter_taps, out_gate, norm_gain.reshape(1, -1), skip_gain.reshape(1, -1), fwd, inv)

    return jax.shard_map(
        local,
        mesh=mesh,
        in_specs=(P("ctx", "ch"), P("ch"), P("ch"), P("ctx", "ch"), P("ctx", "ch")),
        out_specs=P("ctx", "ch"),
        check_vma=False,
    )
```

```python
import functools
import math

import jax
import jax.numpy as jnp
import ml_dtypes
import numpy as np
from jax import lax
from jax.experimental import pallas as pl
from jax.experimental.pallas import tpu as pltpu
from jax.sharding import PartitionSpec as P

C = 8192
EPS = 1e-06
MESH = pl.DeviceIdType.MESH
STEP = 8


def high_low(table):
    high = table.astype(ml_dtypes.bfloat16)
    low = (table - high.astype(np.float64)).astype(ml_dtypes.bfloat16)
    return high, low


def dft_tables(rows):
    span = 2 * rows
    freq = np.arange(rows)

    def phase(a, b):
        return (a[:, None] * b[None, :] % span) * (2.0 * math.pi / span)

    row = np.arange(rows)
    angle = phase(row, freq)
    fwd_im = -np.sin(angle)
    fwd_im[:, 0] = np.cos(math.pi * row)
    forward = np.concatenate([np.cos(angle), fwd_im], axis=1)
    out = np.arange(span)
    angle = phase(freq, out)
    inv_re = 2.0 * np.cos(angle) / span
    inv_re[0] = 1.0 / span
    inv_im = -2.0 * np.sin(angle) / span
    inv_im[0] = np.cos(math.pi * out) / span
    high, low = high_low(np.concatenate([inv_re, inv_im], axis=0))
    return np.concatenate(high_low(forward), axis=0), np.concatenate([high, high, low], axis=0)


def kernel(
    n_ctx, n_ch, channels_all,
    sig_hbm, tap_hbm, gate_hbm, gain_hbm, skip_hbm, fwd_hbm, inv_hbm, out_ref,
    sig, tap, gate, gain, skip, fwd, inv, load_sem,
    part, part_send, part_recv,
    tap_out, tap_relay, tap_in, x_out, x_in, back_out, back_in,
    send_sem, recv_sem, relay_send, relay_recv, pass_send, far_sem,
    normed, turned, spec_x, spec_h, spec_y,
):
    rows, chans = sig.shape
    cpd = chans // n_ctx
    half = cpd // 2
    me = lax.axis_index("ctx")
    me_ch = lax.axis_index("ch")
    chip, core, n_chips = me // 2, lax.rem(me, 2), n_ctx // 2
    reach, turn = n_chips // 4, n_chips // 2
    relayed = 2 * (turn - reach) - 1

    loads = [
        pltpu.make_async_copy(src, dst, load_sem.at[k])
        for k, (src, dst) in enumerate(
            (
                (sig_hbm, sig), (tap_hbm, tap), (gain_hbm, gain), (fwd_hbm, fwd),
                (inv_hbm, inv), (gate_hbm, gate), (skip_hbm, skip),
            )
        )
    ]

    barrier = pltpu.get_barrier_semaphore()

    def chip_away(far, right):
        return lax.rem(jnp.where(right, chip + far, chip + n_chips - far), n_chips)

    def over_ctx(action):
        def step(n, _):
            q = n // 2
            peer_chip = chip_away(turn - (q + 1) // 2, q % 2 == 1)
            action(2 * peer_chip + jnp.where(n < n_ctx - 2, n % 2, 1 - core))
            return 0

        lax.fori_loop(0, n_ctx - 1, step, 0)

    def over_near(action):
        def step(n, _):
            peer_chip = chip_away(reach - n // 4, (n // 2) % 2 == 1)
            action(2 * peer_chip + jnp.where(n < 4 * reach, n % 2, 1 - core))
            return 0

        lax.fori_loop(0, 4 * reach + 1, step, 0)

    def over_ch(action):
        def step(d, _):
            action(lax.rem(me_ch + d, n_ch))
            return 0

        lax.fori_loop(1, n_ch, step, 0)

    def part_copy(peer, slot):
        return pltpu.make_async_remote_copy(
            src_ref=part.at[me_ch], dst_ref=part.at[slot], send_sem=part_send.at[peer], recv_sem=part_recv.at[slot],
            device_id={"ch": peer}, device_id_type=MESH,
        )

    def tile_copy(source, target, k, peer):
        return pltpu.make_async_remote_copy(
            src_ref=source.at[peer], dst_ref=target.at[me], send_sem=send_sem.at[k], recv_sem=recv_sem.at[k],
            device_id={"ctx": peer}, device_id_type=MESH,
        )

    def half_copy(source, target, k, peer):
        return pltpu.make_async_remote_copy(
            src_ref=source, dst_ref=target, send_sem=send_sem.at[k], recv_sem=recv_sem.at[k],
            device_id={"ctx": peer}, device_id_type=MESH,
        )

    def halves_of(source, target, k):
        return half_copy(source, target, k, lax.rem(me + 1, n_ctx))

    def tiles_of(target, count, k):
        return pltpu.make_async_remote_copy(
            src_ref=target.at[pl.ds(0, count)], dst_ref=target.at[pl.ds(0, count)],
            send_sem=send_sem.at[k], recv_sem=recv_sem.at[k],
            device_id={"ctx": lax.rem(me + 1, n_ctx)}, device_id_type=MESH,
        )

    def relay_copy(source, relay, k, side):
        far_first = 2 * chip_away(reach + 1, True) if side == 0 else 2 * chip_away(turn, False) + 1
        return pltpu.make_async_remote_copy(
            src_ref=source.at[pl.ds(far_first, relayed)], dst_ref=relay.at[side],
            send_sem=relay_send.at[side], recv_sem=relay_recv.at[side],
            device_id={"ctx": 2 * chip_away(reach, side == 0) + core}, device_id_type=MESH,
        )

    def pass_on(relay, target, k, side, action):
        origin = 2 * chip_away(reach, side == 1) + core
        far_first = 2 * (chip + 1) if side == 0 else 2 * (chip + n_chips + reach - turn) + 1

        def step(t, _):
            action(
                pltpu.make_async_remote_copy(
                    src_ref=relay.at[side, t], dst_ref=target.at[origin],
                    send_sem=pass_send, recv_sem=recv_sem.at[k],
                    device_id={"ctx": lax.rem(far_first + t, n_ctx)}, device_id_type=MESH,
                )
            )
            return 0

        lax.fori_loop(0, relayed, step, 0)

    def send_tiles(source, relay, target, k):
        for side in range(2):
            relay_copy(source, relay, k, side).start()
        over_near(lambda peer: tile_copy(source, target, k, peer).start())
        target[pl.ds(me, 1)] = source[pl.ds(me, 1)]

    def forward_tiles(source, relay, target, k):
        for side in range(2):
            relay_copy(source, relay, k, side).wait_recv()
            pass_on(relay, target, k, side, lambda copy: copy.start())

    over_near(lambda peer: pl.semaphore_signal(barrier, inc=1, device_id={"ctx": peer}, device_id_type=MESH))
    over_ch(lambda peer: pl.semaphore_signal(barrier, inc=1, device_id={"ch": peer}, device_id_type=MESH))
    for load in loads:
        load.start()

    loads[0].wait()
    values = sig[...].astype(jnp.float32)
    squares = values * values
    lanes = squares[:, :128]
    for k in range(1, chans // 128):
        lanes += squares[:, k * 128 : (k + 1) * 128]
    part[pl.ds(me_ch, 1)] = jnp.sum(lanes.T, axis=0, keepdims=True).reshape(1, 1, rows)
    loads[1].wait()
    tap_tiles = tap[...].astype(jnp.float32).T.astype(jnp.bfloat16).reshape(n_ctx, cpd, rows)
    tap_out[:n_ctx] = tap_tiles
    tap_out[n_ctx:] = tap_tiles

    pl.semaphore_wait(barrier, 4 * reach + 1 + n_ch - 1)
    for right in (True, False):
        pl.semaphore_signal(
            far_sem, inc=1, device_id={"ctx": 2 * chip_away(reach, right) + core}, device_id_type=MESH
        )
    over_ch(lambda peer: part_copy(peer, me_ch).start())
    send_tiles(tap_out, tap_relay, tap_in, 0)

    loads[2].wait()
    turned[...] = (values * gain[...]).T
    over_ch(lambda peer: part_copy(peer, peer).wait_recv())
    scale = lax.rsqrt(jnp.sum(part[...], axis=0) / channels_all + EPS)
    x_out[...] = (turned[...] * scale).reshape(n_ctx, 2, half, rows).astype(jnp.bfloat16)
    pl.semaphore_wait(far_sem, 2)
    for part_no in range(2):
        over_ctx(lambda peer: half_copy(x_out.at[peer, part_no], x_in.at[part_no, me], 1 + part_no, peer).start())
        x_in[part_no, pl.ds(me, 1)] = x_out[pl.ds(me, 1), part_no]
    forward_tiles(tap_out, tap_relay, tap_in, 0)
    column = jnp.broadcast_to(scale, (128, rows)).T
    for k in range(chans // 128):
        at = pl.ds(k * 128, 128)
        normed[:, at] = (sig[:, at].astype(jnp.float32) * gain[:, at] * column).astype(jnp.bfloat16)

    def spectrum(tiles):
        lines = tiles.reshape(-1, rows)
        both = jnp.concatenate([lines, lines], axis=1)
        whole = jnp.dot(both, fwd[...], preferred_element_type=jnp.float32).reshape(n_ctx, -1, 2 * rows)
        re, im = whole[:, :, :rows], whole[:, :, rows:]
        return re, im, re + im

    spec_h[:, :STEP] = jnp.zeros((3, STEP, cpd, rows), jnp.float32)
    loads[3].wait()
    tiles_of(tap_in, n_ctx - 1, 0).wait_recv()
    for k, values in enumerate(spectrum(tap_in[...])):
        spec_h[k, STEP:] = values
    loads[4].wait()

    lane = lax.broadcasted_iota(jnp.int32, (half, rows), 1)

    for part_no in range(2):
        sub = pl.ds(part_no * half, half)
        halves_of(x_in.at[part_no, pl.ds(0, n_ctx - 1)], x_in.at[part_no, pl.ds(0, n_ctx - 1)], 1 + part_no).wait_recv()
        lines = x_in[part_no].astype(jnp.float32).reshape(n_ctx * half, rows).astype(jnp.bfloat16)
        for k, values in enumerate(spectrum(lines)):
            spec_x[k] = values

        def convolve(n, _):
            def add_blocks(m, sums):
                sums = list(sums)
                base = (n - m) * STEP
                for b in range(STEP):
                    x = [spec_x[k, m * STEP + b] for k in range(3)]
                    for a in range(STEP):
                        for k in range(3):
                            sums[3 * a + k] += x[k] * spec_h[k, base + a - b + STEP, sub, :]
                return tuple(sums)

            blank = jnp.zeros((half, rows), jnp.float32)
            sums = lax.fori_loop(0, n + 1, add_blocks, (blank,) * (3 * STEP))
            for a in range(STEP):
                re, im, both = sums[3 * a : 3 * a + 3]
                spec_y[n * STEP + a, :, :rows] = jnp.where(lane == 0, re, re - im)
                spec_y[n * STEP + a, :, rows:] = jnp.where(lane == 0, im, both - re - im)
            return 0

        lax.fori_loop(0, n_ctx // STEP, convolve, 0)
        wave = spec_y[...].reshape(n_ctx * half, 2 * rows)
        high = wave.astype(jnp.bfloat16)
        low = (wave - high.astype(jnp.float32)).astype(jnp.bfloat16)
        time = jnp.dot(
            jnp.concatenate([high, low, high], axis=1), inv[...], preferred_element_type=jnp.float32
        ).reshape(n_ctx, half, 2 * rows)
        early, late = time[:, :, :rows], time[:, :, rows:]
        back_out[part_no] = (
            early + jnp.concatenate([jnp.zeros((1, half, rows), jnp.float32), late[: n_ctx - 1]], axis=0)
        ).astype(jnp.bfloat16)
        over_ctx(lambda peer: half_copy(back_out.at[part_no, peer], back_in.at[me, part_no], 3 + part_no, peer).start())
        back_in[pl.ds(me, 1), part_no] = back_out[part_no, pl.ds(me, 1)]

    loads[5].wait()
    loads[6].wait()
    direct = skip[...] * normed[...].astype(jnp.float32)
    some_back = back_in.at[pl.ds(0, n_ctx - 1), 0]
    for part_no in range(2):
        halves_of(back_out.at[part_no, pl.ds(0, n_ctx - 1)], some_back, 3 + part_no).wait_recv()
    result = back_in[...].astype(jnp.float32).reshape(chans, rows).T
    out_ref[...] = (gate[...].astype(jnp.float32) * (result + direct)).astype(jnp.bfloat16)

    over_ch(lambda peer: part_copy(peer, me_ch).wait_send())
    tiles_of(tap_in, 4 * reach + 1, 0).wait_send()
    for side in range(2):
        relay_copy(tap_out, tap_relay, 0, side).wait_send()
        pass_on(tap_relay, tap_in, 0, side, lambda copy: copy.wait_send())
    some_x = x_in.at[0, pl.ds(0, n_ctx - 1)]
    for k in range(1, 5):
        halves_of(some_x, some_x, k).wait_send()


def solution(mesh):
    n_ctx, n_ch = mesh.shape["ctx"], mesh.shape["ch"]

    def local(signal, norm_gain, skip_gain, filter_taps, out_gate):
        rows, chans = signal.shape
        cpd = chans // n_ctx
        fwd, inv = (jnp.asarray(table) for table in dft_tables(rows))
        f32, bf16 = jnp.float32, jnp.bfloat16
        vmem, dma = pltpu.VMEM, pltpu.SemaphoreType.DMA
        hbm = pl.BlockSpec(memory_space=pltpu.HBM)
        block, tiles = vmem((rows, chans), bf16), vmem((n_ctx, cpd, rows), bf16)
        twice = vmem((2 * n_ctx, cpd, rows), bf16)
        relay = vmem((2, 2 * (n_ctx // 4 - n_ctx // 8) - 1, cpd, rows), bf16)
        return pl.pallas_call(
            functools.partial(kernel, n_ctx, n_ch, chans * n_ch),
            out_shape=jax.ShapeDtypeStruct((rows, chans), bf16),
            in_specs=[hbm] * 7,
            out_specs=pl.BlockSpec(memory_space=pltpu.VMEM),
            scratch_shapes=[
                block, block, block, vmem((1, chans), f32), vmem((1, chans), f32),
                vmem(fwd.shape, bf16), vmem(inv.shape, bf16), dma((7,)),
                vmem((n_ch, 1, rows), f32), dma((n_ch,)), dma((n_ch,)),
                twice, relay, tiles, vmem((n_ctx, 2, cpd // 2, rows), bf16), vmem((2, n_ctx, cpd // 2, rows), bf16),
                vmem((2, n_ctx, cpd // 2, rows), bf16), vmem((n_ctx, 2, cpd // 2, rows), bf16),
                dma((5,)), dma((5,)), dma((2,)), dma((2,)), dma(()), pltpu.SemaphoreType.REGULAR,
                block, vmem((chans, rows), f32), vmem((3, n_ctx, cpd // 2, rows), f32), vmem((3, n_ctx + STEP, cpd, rows), f32),
                vmem((n_ctx, cpd // 2, 2 * rows), f32),
            ],
            compiler_params=pltpu.CompilerParams(
                collective_id=0, has_side_effects=True, vmem_limit_bytes=62 * 1024 * 1024
            ),
        )(signal, filter_taps, out_gate, norm_gain.reshape(1, -1), skip_gain.reshape(1, -1), fwd, inv)

    return jax.shard_map(
        local,
        mesh=mesh,
        in_specs=(P("ctx", "ch"), P("ch"), P("ch"), P("ctx", "ch"), P("ctx", "ch")),
        out_specs=P("ctx", "ch"),
        check_vma=False,
    )
```

```python
import functools
import math

import jax
import jax.numpy as jnp
import ml_dtypes
import numpy as np
from jax import lax
from jax.experimental import pallas as pl
from jax.experimental.pallas import tpu as pltpu
from jax.sharding import PartitionSpec as P

C = 8192
EPS = 1e-06
MESH = pl.DeviceIdType.MESH
STEP = 8


def high_low(table):
    high = table.astype(ml_dtypes.bfloat16)
    low = (table - high.astype(np.float64)).astype(ml_dtypes.bfloat16)
    return high, low


def dft_tables(rows):
    span = 2 * rows
    freq = np.arange(rows)

    def phase(a, b):
        return (a[:, None] * b[None, :] % span) * (2.0 * math.pi / span)

    row = np.arange(rows)
    angle = phase(row, freq)
    fwd_im = -np.sin(angle)
    fwd_im[:, 0] = np.cos(math.pi * row)
    forward = np.concatenate([np.cos(angle), fwd_im], axis=1)
    out = np.arange(span)
    angle = phase(freq, out)
    inv_re = 2.0 * np.cos(angle) / span
    inv_re[0] = 1.0 / span
    inv_im = -2.0 * np.sin(angle) / span
    inv_im[0] = np.cos(math.pi * out) / span
    high, low = high_low(np.concatenate([inv_re, inv_im], axis=0))
    return np.concatenate(high_low(forward), axis=0), np.concatenate([high, high, low], axis=0)


def kernel(
    n_ctx, n_ch, channels_all,
    sig_hbm, tap_hbm, gate_hbm, gain_hbm, skip_hbm, fwd_hbm, inv_hbm, out_ref,
    sig, tap, gate, gain, skip, fwd, inv, load_sem,
    part, part_send, part_recv,
    tap_out, tap_relay, tap_in, x_out, x_in, back_out, back_in,
    send_sem, recv_sem, relay_send, relay_recv, pass_send, far_sem,
    normed, turned, spec_x, spec_h, spec_y,
):
    rows, chans = sig.shape
    cpd = chans // n_ctx
    half = cpd // 2
    me = lax.axis_index("ctx")
    me_ch = lax.axis_index("ch")
    chip, core, n_chips = me // 2, lax.rem(me, 2), n_ctx // 2
    reach, turn = n_chips // 4, n_chips // 2
    relayed = 2 * (turn - reach) - 1

    loads = [
        pltpu.make_async_copy(src, dst, load_sem.at[k])
        for k, (src, dst) in enumerate(
            (
                (sig_hbm, sig), (tap_hbm, tap), (gain_hbm, gain), (fwd_hbm, fwd),
                (inv_hbm, inv), (gate_hbm, gate), (skip_hbm, skip),
            )
        )
    ]

    barrier = pltpu.get_barrier_semaphore()

    def chip_away(far, right):
        return lax.rem(jnp.where(right, chip + far, chip + n_chips - far), n_chips)

    def over_ctx(action):
        def step(n, _):
            q = n // 2
            peer_chip = chip_away(turn - (q + 1) // 2, q % 2 == 1)
            action(2 * peer_chip + jnp.where(n < n_ctx - 2, n % 2, 1 - core))
            return 0

        lax.fori_loop(0, n_ctx - 1, step, 0)

    def over_near(action):
        def step(n, _):
            peer_chip = chip_away(reach - n // 4, (n // 2) % 2 == 1)
            action(2 * peer_chip + jnp.where(n < 4 * reach, n % 2, 1 - core))
            return 0

        lax.fori_loop(0, 4 * reach + 1, step, 0)

    def over_ch(action):
        def step(d, _):
            action(lax.rem(me_ch + d, n_ch))
            return 0

        lax.fori_loop(1, n_ch, step, 0)

    def part_copy(peer, slot):
        return pltpu.make_async_remote_copy(
            src_ref=part.at[me_ch], dst_ref=part.at[slot], send_sem=part_send.at[peer], recv_sem=part_recv.at[slot],
            device_id={"ch": peer}, device_id_type=MESH,
        )

    def tile_copy(source, target, k, peer):
        return pltpu.make_async_remote_copy(
            src_ref=source.at[peer], dst_ref=target.at[me], send_sem=send_sem.at[k], recv_sem=recv_sem.at[k],
            device_id={"ctx": peer}, device_id_type=MESH,
        )

    def half_copy(source, target, k, peer):
        return pltpu.make_async_remote_copy(
            src_ref=source, dst_ref=target, send_sem=send_sem.at[k], recv_sem=recv_sem.at[k],
            device_id={"ctx": peer}, device_id_type=MESH,
        )

    def halves_of(source, target, k):
        return half_copy(source, target, k, lax.rem(me + 1, n_ctx))

    def tiles_of(target, count, k):
        return pltpu.make_async_remote_copy(
            src_ref=target.at[pl.ds(0, count)], dst_ref=target.at[pl.ds(0, count)],
            send_sem=send_sem.at[k], recv_sem=recv_sem.at[k],
            device_id={"ctx": lax.rem(me + 1, n_ctx)}, device_id_type=MESH,
        )

    def relay_copy(source, relay, k, side):
        far_first = 2 * chip_away(reach + 1, True) if side == 0 else 2 * chip_away(turn, False) + 1
        return pltpu.make_async_remote_copy(
            src_ref=source.at[pl.ds(far_first, relayed)], dst_ref=relay.at[side],
            send_sem=relay_send.at[side], recv_sem=relay_recv.at[side],
            device_id={"ctx": 2 * chip_away(reach, side == 0) + core}, device_id_type=MESH,
        )

    def pass_on(relay, target, k, side, action):
        origin = 2 * chip_away(reach, side == 1) + core
        far_first = 2 * (chip + 1) if side == 0 else 2 * (chip + n_chips + reach - turn) + 1

        def step(t, _):
            action(
                pltpu.make_async_remote_copy(
                    src_ref=relay.at[side, t], dst_ref=target.at[origin],
                    send_sem=pass_send, recv_sem=recv_sem.at[k],
                    device_id={"ctx": lax.rem(far_first + t, n_ctx)}, device_id_type=MESH,
                )
            )
            return 0

        lax.fori_loop(0, relayed, step, 0)

    def send_tiles(source, relay, target, k):
        for side in range(2):
            relay_copy(source, relay, k, side).start()
        over_near(lambda peer: tile_copy(source, target, k, peer).start())
        target[pl.ds(me, 1)] = source[pl.ds(me, 1)]

    def forward_tiles(source, relay, target, k):
        for side in range(2):
            relay_copy(source, relay, k, side).wait_recv()
            pass_on(relay, target, k, side, lambda copy: copy.start())

    over_near(lambda peer: pl.semaphore_signal(barrier, inc=1, device_id={"ctx": peer}, device_id_type=MESH))
    over_ch(lambda peer: pl.semaphore_signal(barrier, inc=1, device_id={"ch": peer}, device_id_type=MESH))
    for load in loads:
        load.start()

    loads[0].wait()
    values = sig[...].astype(jnp.float32)
    squares = values * values
    lanes = squares[:, :128]
    for k in range(1, chans // 128):
        lanes += squares[:, k * 128 : (k + 1) * 128]
    part[pl.ds(me_ch, 1)] = jnp.sum(lanes.T, axis=0, keepdims=True).reshape(1, 1, rows)
    loads[1].wait()
    tap_tiles = tap[...].astype(jnp.float32).T.astype(jnp.bfloat16).reshape(n_ctx, cpd, rows)
    tap_out[:n_ctx] = tap_tiles
    tap_out[n_ctx:] = tap_tiles

    pl.semaphore_wait(barrier, 4 * reach + 1 + n_ch - 1)
    for right in (True, False):
        pl.semaphore_signal(
            far_sem, inc=1, device_id={"ctx": 2 * chip_away(reach, right) + core}, device_id_type=MESH
        )
    over_ch(lambda peer: part_copy(peer, me_ch).start())
    send_tiles(tap_out, tap_relay, tap_in, 0)

    loads[2].wait()
    turned[...] = (values * gain[...]).T
    over_ch(lambda peer: part_copy(peer, peer).wait_recv())
    scale = lax.rsqrt(jnp.sum(part[...], axis=0) / channels_all + EPS)
    x_out[...] = (turned[...] * scale).reshape(n_ctx, 2, half, rows).astype(jnp.bfloat16)
    pl.semaphore_wait(far_sem, 2)
    for part_no in range(2):
        over_ctx(lambda peer: half_copy(x_out.at[peer, part_no], x_in.at[part_no, me], 1 + part_no, peer).start())
        x_in[part_no, pl.ds(me, 1)] = x_out[pl.ds(me, 1), part_no]
    forward_tiles(tap_out, tap_relay, tap_in, 0)
    column = jnp.broadcast_to(scale, (128, rows)).T
    for k in range(chans // 128):
        at = pl.ds(k * 128, 128)
        normed[:, at] = (sig[:, at].astype(jnp.float32) * gain[:, at] * column).astype(jnp.bfloat16)

    def spectrum(tiles):
        lines = tiles.reshape(-1, rows)
        both = jnp.concatenate([lines, lines], axis=1)
        whole = jnp.dot(both, fwd[...], preferred_element_type=jnp.float32).reshape(n_ctx, -1, 2 * rows)
        re, im = whole[:, :, :rows], whole[:, :, rows:]
        return re, im, re + im

    spec_h[:, :STEP] = jnp.zeros((3, STEP, cpd, rows), jnp.float32)
    loads[3].wait()
    tiles_of(tap_in, n_ctx - 1, 0).wait_recv()
    for k, values in enumerate(spectrum(tap_in[...])):
        spec_h[k, STEP:] = values
    loads[4].wait()

    lane = lax.broadcasted_iota(jnp.int32, (half, rows), 1)

    for part_no in range(2):
        sub = pl.ds(part_no * half, half)
        halves_of(x_in.at[part_no, pl.ds(0, n_ctx - 1)], x_in.at[part_no, pl.ds(0, n_ctx - 1)], 1 + part_no).wait_recv()
        lines = x_in[part_no].astype(jnp.float32).reshape(n_ctx * half, rows).astype(jnp.bfloat16)
        for k, values in enumerate(spectrum(lines)):
            spec_x[k] = values

        def convolve(n, _):
            def add_blocks(m, sums):
                sums = list(sums)
                base = (n - m) * STEP
                for b in range(STEP):
                    x = [spec_x[k, m * STEP + b] for k in range(3)]
                    for a in range(STEP):
                        for k in range(3):
                            sums[3 * a + k] += x[k] * spec_h[k, base + a - b + STEP, sub, :]
                return tuple(sums)

            blank = jnp.zeros((half, rows), jnp.float32)
            sums = lax.fori_loop(0, n + 1, add_blocks, (blank,) * (3 * STEP))
            for a in range(STEP):
                re, im, both = sums[3 * a : 3 * a + 3]
                spec_y[n * STEP + a, :, :rows] = jnp.where(lane == 0, re, re - im)
                spec_y[n * STEP + a, :, rows:] = jnp.where(lane == 0, im, both - re - im)
            return 0

        lax.fori_loop(0, n_ctx // STEP, convolve, 0)
        wave = spec_y[...].reshape(n_ctx * half, 2 * rows)
        high = wave.astype(jnp.bfloat16)
        low = (wave - high.astype(jnp.float32)).astype(jnp.bfloat16)
        time = jnp.dot(
            jnp.concatenate([high, low, high], axis=1), inv[...], preferred_element_type=jnp.float32
        ).reshape(n_ctx, half, 2 * rows)
        early, late = time[:, :, :rows], time[:, :, rows:]
        back_out[part_no] = (
            early + jnp.concatenate([jnp.zeros((1, half, rows), jnp.float32), late[: n_ctx - 1]], axis=0)
        ).astype(jnp.bfloat16)
        over_ctx(lambda peer: half_copy(back_out.at[part_no, peer], back_in.at[me, part_no], 3 + part_no, peer).start())
        back_in[pl.ds(me, 1), part_no] = back_out[part_no, pl.ds(me, 1)]

    loads[5].wait()
    loads[6].wait()
    direct = skip[...] * normed[...].astype(jnp.float32)
    over_ch(lambda peer: part_copy(peer, me_ch).wait_send())
    tiles_of(tap_in, 4 * reach + 1, 0).wait_send()
    for side in range(2):
        relay_copy(tap_out, tap_relay, 0, side).wait_send()
        pass_on(tap_relay, tap_in, 0, side, lambda copy: copy.wait_send())
    some_x = x_in.at[0, pl.ds(0, n_ctx - 1)]
    for k in range(1, 5):
        halves_of(some_x, some_x, k).wait_send()
    some_back = back_in.at[pl.ds(0, n_ctx - 1), 0]
    for part_no in range(2):
        halves_of(back_out.at[part_no, pl.ds(0, n_ctx - 1)], some_back, 3 + part_no).wait_recv()
    result = back_in[...].astype(jnp.float32).reshape(chans, rows).T
    out_ref[...] = (gate[...].astype(jnp.float32) * (result + direct)).astype(jnp.bfloat16)


def solution(mesh):
    n_ctx, n_ch = mesh.shape["ctx"], mesh.shape["ch"]

    def local(signal, norm_gain, skip_gain, filter_taps, out_gate):
        rows, chans = signal.shape
        cpd = chans // n_ctx
        fwd, inv = (jnp.asarray(table) for table in dft_tables(rows))
        f32, bf16 = jnp.float32, jnp.bfloat16
        vmem, dma = pltpu.VMEM, pltpu.SemaphoreType.DMA
        hbm = pl.BlockSpec(memory_space=pltpu.HBM)
        block, tiles = vmem((rows, chans), bf16), vmem((n_ctx, cpd, rows), bf16)
        twice = vmem((2 * n_ctx, cpd, rows), bf16)
        relay = vmem((2, 2 * (n_ctx // 4 - n_ctx // 8) - 1, cpd, rows), bf16)
        return pl.pallas_call(
            functools.partial(kernel, n_ctx, n_ch, chans * n_ch),
            out_shape=jax.ShapeDtypeStruct((rows, chans), bf16),
            in_specs=[hbm] * 7,
            out_specs=pl.BlockSpec(memory_space=pltpu.VMEM),
            scratch_shapes=[
                block, block, block, vmem((1, chans), f32), vmem((1, chans), f32),
                vmem(fwd.shape, bf16), vmem(inv.shape, bf16), dma((7,)),
                vmem((n_ch, 1, rows), f32), dma((n_ch,)), dma((n_ch,)),
                twice, relay, tiles, vmem((n_ctx, 2, cpd // 2, rows), bf16), vmem((2, n_ctx, cpd // 2, rows), bf16),
                vmem((2, n_ctx, cpd // 2, rows), bf16), vmem((n_ctx, 2, cpd // 2, rows), bf16),
                dma((5,)), dma((5,)), dma((2,)), dma((2,)), dma(()), pltpu.SemaphoreType.REGULAR,
                block, vmem((chans, rows), f32), vmem((3, n_ctx, cpd // 2, rows), f32), vmem((3, n_ctx + STEP, cpd, rows), f32),
                vmem((n_ctx, cpd // 2, 2 * rows), f32),
            ],
            compiler_params=pltpu.CompilerParams(
                collective_id=0, has_side_effects=True, vmem_limit_bytes=62 * 1024 * 1024
            ),
        )(signal, filter_taps, out_gate, norm_gain.reshape(1, -1), skip_gain.reshape(1, -1), fwd, inv)

    return jax.shard_map(
        local,
        mesh=mesh,
        in_specs=(P("ctx", "ch"), P("ch"), P("ch"), P("ctx", "ch"), P("ctx", "ch")),
        out_specs=P("ctx", "ch"),
        check_vma=False,
    )
```
